32 devices in a mesh: dp: 8 (over z, y), head: 4 (over x, core).
Axes of the slice: x: 2, y: 2, z: 4, core: 2. Of those that a mesh axis runs over, the one named last changes fastest.
Arguments:
- tokens: bfloat16 [32768, 768], P(('dp', 'head')), may hold values from -6 to 6
- seq_lengths: int32 [8], P('dp'), may hold values from 128 to 4096, as said below
- seg_bounds: int32 [8, 65], P('dp'), may hold values from 0 to 4096, as said below
- w_qkv: bfloat16 [768, 2304], replicated, may hold values from -0.625 to 0.625
- b_qv: float32 [1536], replicated, may hold values from -6 to 6
- conv_w: float32 [12, 33], P('head'), may hold values from -0.3 to 0.3
- w_out: bfloat16 [768, 768], replicated, may hold values from -0.4375 to 0.4375
- b_out: float32 [768], replicated, may hold values from -3 to 3
- ln1_gain: float32 [768], replicated, may hold values from 0.5 to 1.5
- ln1_bias: float32 [768], replicated, may hold values from -3 to 3
- w_up: bfloat16 [768, 3072], replicated, may hold values from -0.21875 to 0.21875
- b_up: float32 [3072], replicated, may hold values from -3 to 3
- w_down: bfloat16 [3072, 768], replicated, may hold values from -0.109375 to 0.109375
- b_down: float32 [768], replicated, may hold values from -3 to 3
- ln2_gain: float32 [768], replicated, may hold values from 0.5 to 1.5
- ln2_bias: float32 [768], replicated, may hold values from -3 to 3
- cotangent: bfloat16 [32768, 768], P(('dp', 'head')), may hold values from -6 to 6
Outputs:
- out: bfloat16 [32768, 768], P(('dp', 'head'))
- grad_tokens: float32 [32768, 768], P(('dp', 'head'))
- grad_w_qkv: float32 [768, 2304], replicated
- grad_b_qv: float32 [1536], replicated
- grad_conv_w: float32 [12, 33], P('head')
- grad_w_out: float32 [768, 768], replicated
- grad_b_out: float32 [768], replicated
- grad_ln1_gain: float32 [768], replicated
- grad_ln1_bias: float32 [768], replicated
- grad_w_up: float32 [768, 3072], replicated
- grad_b_up: float32 [3072], replicated
- grad_w_down: float32 [3072, 768], replicated
- grad_b_down: float32 [768], replicated
- grad_ln2_gain: float32 [768], replicated
- grad_ln2_bias: float32 [768], replicated
- pinv_residual: float32 [8, 12], P('dp', 'head')
The draws below stay inside these ranges and needn't reach their ends.
Inputs may be any that keep to these rules, and one draw needn't show every extreme that they name: Sequence s holds seq_lengths[s] real tokens at the start of its 4096 positions; the rest is padding. `seg_bounds`: row s rises strictly from 0 to seq_lengths[s]; every landmark segment holds one or more positions.
All inputs are finite; a program needn't handle non-finite values.
Results may differ from the reference program's by a relative error of at most 0.014.
The reference program's roundings to bfloat16 on the way count: a program that leaves them out, or rounds other values in their place, can miss the bound.
Values may be sent and summed in bfloat16 or wider, within the bound.
No kernel may reach another device: no remote copies, remote signals or barrier semaphores. Data moves between devices by JAX's collectives and lax.ppermute only.
A program may use at most 320 MiB of HBM per device.

```python
import jax
import jax.numpy as jnp
from jax import lax

D = 768
HEADS = 12
FF = 3072
LAND = 64
KERNEL = 33
ITERS = 6
BUCKET = 4096
MIN_LEN = 128
SEQ_GRP = 1
SEQS = 8
TOKENS = 32768


def make_lengths(key):
    drawn = jax.random.randint(jax.random.fold_in(key, 11), (SEQS,), MIN_LEN, BUCKET + 1, dtype=jnp.int32)
    drawn = drawn.at[0].set(BUCKET)
    return drawn.at[1].set(MIN_LEN)


def draw_seq_lengths(key, part):
    return make_lengths(key)


def draw_seg_bounds(key, part):
    lengths = make_lengths(key)
    widths_drawn = jax.random.randint(jax.random.fold_in(key, 12), (SEQS, LAND), 2, 4, dtype=jnp.int32)
    running = jnp.concatenate([jnp.zeros((SEQS, 1), jnp.int32), jnp.cumsum(widths_drawn, axis=1)], axis=1)
    totals = running[:, -1:]
    return lengths[:, None] * running // totals


def shard_levels(rng, extent, split, low, largest):
    def one(axis_at, shards_of):
        draws = jax.random.uniform(jax.random.fold_in(jax.random.fold_in(rng, 6), axis_at), (shards_of,), jnp.float32, low / len(split), largest / len(split))
        return jnp.repeat(jnp.exp(draws), extent[axis_at] // shards_of).reshape((-1,) + (1,) * (len(extent) - axis_at - 1))

    factor_of = one(*split[0])
    for cut in split[1:]:
        factor_of = factor_of * one(*cut)
    return factor_of


def noise(stream_key, extent, scale, most, shards=(), kind=jnp.bfloat16):
    loudness = shard_levels(stream_key, extent, shards, -0.22, 0.18) if shards else 1.0
    values = jax.random.normal(stream_key, extent, jnp.float32) * scale * loudness
    return jnp.minimum(jnp.maximum(values, -most), most).astype(kind)


def setup_inputs(seed: int = 0) -> dict:
    streams_of = jax.random.split(jax.random.key(seed), 18)
    tokens = noise(streams_of[0], (TOKENS, D), 1.0, 6.0, ((0, 32),))
    seq_lengths = draw_seq_lengths(jax.random.fold_in(streams_of[17], 71), 0)
    seg_bounds = draw_seg_bounds(jax.random.fold_in(streams_of[17], 71), 0)
    w_qkv = noise(streams_of[3], (D, 3 * D), (D // 8) ** -0.5, 0.625)
    b_qv = noise(streams_of[4], (2 * D,), 1.0, 6.0, (), jnp.float32)
    conv_w = noise(streams_of[5], (HEADS, KERNEL), 0.05, 0.3, ((0, 4),), jnp.float32)
    w_out = noise(streams_of[6], (D, D), (D // 4) ** -0.5, 0.4375)
    b_out = noise(streams_of[7], (D,), 0.5, 3.0, (), jnp.float32)
    ln1_gain = jnp.clip(1.0 + 0.1 * jax.random.normal(streams_of[8], (D,), jnp.float32), 0.5, 1.5)
    ln1_bias = noise(streams_of[9], (D,), 0.5, 3.0, (), jnp.float32)
    w_up = noise(streams_of[10], (D, FF), D ** -0.5, 0.21875)
    b_up = noise(streams_of[11], (FF,), 0.5, 3.0, (), jnp.float32)
    w_down = noise(streams_of[12], (FF, D), FF ** -0.5, 0.109375)
    b_down = noise(streams_of[13], (D,), 0.5, 3.0, (), jnp.float32)
    ln2_gain = jnp.clip(1.0 + 0.1 * jax.random.normal(streams_of[14], (D,), jnp.float32), 0.5, 1.5)
    ln2_bias = noise(streams_of[15], (D,), 0.5, 3.0, (), jnp.float32)
    cotangent = noise(streams_of[16], (TOKENS, D), 1.0, 6.0, ((0, 32),))
    return dict(tokens=tokens, seq_lengths=seq_lengths, seg_bounds=seg_bounds, w_qkv=w_qkv, b_qv=b_qv, conv_w=conv_w, w_out=w_out, b_out=b_out, ln1_gain=ln1_gain, ln1_bias=ln1_bias, w_up=w_up, b_up=b_up, w_down=w_down, b_down=b_down, ln2_gain=ln2_gain, ln2_bias=ln2_bias, cotangent=cotangent)


@jax.custom_vjp
def low(v):
    return lax.optimization_barrier(v.astype(jnp.bfloat16)).astype(jnp.float32)

@jax.custom_vjp
def low_back(v):
    return v

def low_keep(v):
    return (low(v), None)

def low_pass(kept, grad):
    return (grad,)

def back_keep(v):
    return (v, None)

def back_low(kept, grad):
    return (low(grad),)
low.defvjp(low_keep, low_pass)
low_back.defvjp(back_keep, back_low)

def layer_norm(inputs, gains, offsets):
    centre = lax.optimization_barrier(jnp.mean(inputs, axis=-1, keepdims=True))
    centred = inputs - centre
    spread = lax.optimization_barrier(jnp.mean(centred * centred, axis=-1, keepdims=True))
    return centred * lax.rsqrt(spread + 1e-05) * gains + offsets

def gelu_exact(inputs):
    return 0.5 * inputs * (1.0 + jax.scipy.special.erf(inputs * 0.7071067811865476))

def pseudo_inverse(kernel):
    highest_precision_flag = lax.Precision.HIGHEST
    landmarks = kernel.shape[-1]
    identity = jnp.eye(landmarks, dtype=kernel.dtype)
    squares = lax.optimization_barrier(jnp.sum(kernel * kernel, axis=(1, 2)))
    inverse_approximation = jnp.swapaxes(kernel, 1, 2) / squares[:, None, None]
    for _ in range(ITERS):
        product = jnp.matmul(kernel, inverse_approximation, precision=highest_precision_flag)
        inner = 7.0 * identity - product
        inner = 15.0 * identity - jnp.matmul(product, inner, precision=highest_precision_flag)
        inner = 13.0 * identity - jnp.matmul(product, inner, precision=highest_precision_flag)
        inverse_approximation = 0.25 * jnp.matmul(inverse_approximation, inner, precision=highest_precision_flag)
    leftover = identity - jnp.matmul(kernel, inverse_approximation, precision=highest_precision_flag)
    residual = jnp.sqrt(lax.optimization_barrier(jnp.sum(leftover * leftover, axis=(1, 2))) / landmarks)
    return (inverse_approximation, residual)

def nystrom(query_matrix, key_matrix, values, length, bounds, taps):
    highest_precision_flag = lax.Precision.HIGHEST
    positions = query_matrix.shape[0]
    scale_factor_term = query_matrix.shape[-1] ** (-0.5)
    position = jnp.arange(positions, dtype=jnp.int32)
    valid = (position < length).astype(jnp.float32)
    member_flags = ((position[None, :] >= bounds[:-1, None]) & (position[None, :] < bounds[1:, None])).astype(jnp.float32)
    valid_count_vector = lax.optimization_barrier(jnp.sum(member_flags, axis=1))
    query_landmark_rows = jnp.einsum('ut,tvr->uvr', member_flags, query_matrix, precision=highest_precision_flag) / valid_count_vector[:, None, None]
    key_landmark_rows = jnp.einsum('ut,tvr->uvr', member_flags, key_matrix, precision=highest_precision_flag) / valid_count_vector[:, None, None]
    first_kernel_matrix = jax.nn.softmax(jnp.einsum('gbw,ubw->bgu', query_matrix, key_landmark_rows, precision=highest_precision_flag) * scale_factor_term, axis=-1)
    middle_kernel_matrix = jax.nn.softmax(jnp.einsum('ouq,puq->uop', query_landmark_rows, key_landmark_rows, precision=highest_precision_flag) * scale_factor_term, axis=-1)
    score_matrix = jnp.einsum('yib,wib->iyw', query_landmark_rows, key_matrix, precision=highest_precision_flag) * scale_factor_term
    score_matrix = jnp.where(valid[None, None, :] > 0.0, score_matrix, -1000000000.0)
    last_kernel_matrix = jax.nn.softmax(score_matrix, axis=-1)
    inverse_approximation, residual = pseudo_inverse(middle_kernel_matrix)
    masked_scores_matrix = values * valid[:, None, None]
    landmark_summary = jnp.einsum('qbl,lqs->qbs', last_kernel_matrix, masked_scores_matrix, precision=highest_precision_flag)
    mixed_value_rows = jnp.einsum('gki,gia->gka', inverse_approximation, landmark_summary, precision=highest_precision_flag)
    attended = jnp.einsum('hnl,hld->nhd', first_kernel_matrix, mixed_value_rows, precision=highest_precision_flag)
    margin = taps.shape[1] // 2
    padded = jnp.pad(masked_scores_matrix, ((margin, margin), (0, 0), (0, 0)))
    convolved = jnp.zeros_like(masked_scores_matrix)
    for tap_index in range(taps.shape[1]):
        convolved = convolved + taps[None, :, tap_index, None] * padded[tap_index:tap_index + positions]
    return ((attended + convolved) * valid[:, None, None], residual)

def group_layer(block_rows, lengths, bounds, params):
    w_qkv, b_qv, conv_w, w_out, b_out, ln1_gain, ln1_bias, w_up, b_up, w_down, b_down, ln2_gain, ln2_bias = params
    highest_precision_flag = lax.Precision.HIGHEST
    width = block_rows.shape[1]
    seq_count = lengths.shape[0]
    bucket = block_rows.shape[0] // seq_count
    heads = conv_w.shape[0]
    qkv_bias = jnp.concatenate([b_qv[:width], jnp.zeros((width,), b_qv.dtype), b_qv[width:]])
    projected = low_back(low(jnp.dot(block_rows, w_qkv, precision=highest_precision_flag) + qkv_bias))
    projected = projected.reshape(seq_count, bucket, 3, heads, width // heads)
    context, residual = jax.vmap(nystrom, in_axes=(0, 0, 0, 0, 0, None))(projected[:, :, 0], projected[:, :, 1], projected[:, :, 2], lengths, bounds, conv_w)
    context = low_back(low(context.reshape(seq_count * bucket, width)))
    attn_out = low_back(jnp.dot(context, w_out, precision=highest_precision_flag) + b_out)
    normed = layer_norm(block_rows + attn_out, ln1_gain, ln1_bias)
    upper = low_back(jnp.dot(low(normed), w_up, precision=highest_precision_flag) + b_up)
    activated = low(gelu_exact(upper))
    ffn_out = low_back(jnp.dot(activated, w_down, precision=highest_precision_flag) + b_down)
    final = layer_norm(normed + ffn_out, ln2_gain, ln2_bias)
    position = jnp.arange(seq_count * bucket, dtype=jnp.int32)
    limit = jnp.repeat(lengths, bucket)
    valid = (position % bucket < limit).astype(jnp.float32)
    return (final * valid[:, None], residual)

def reference(tokens, seq_lengths, seg_bounds, w_qkv, b_qv, conv_w, w_out, b_out, ln1_gain, ln1_bias, w_up, b_up, w_down, b_down, ln2_gain, ln2_bias, cotangent):
    groups = seq_lengths.shape[0] // SEQ_GRP
    params = tuple((item.astype(jnp.float32) for item in (w_qkv, b_qv, conv_w, w_out, b_out, ln1_gain, ln1_bias, w_up, b_up, w_down, b_down, ln2_gain, ln2_bias)))
    inputs = tokens.astype(jnp.float32)

    def forward(token_rows, weights):

        def one_group(item):
            block_rows, lengths, bounds = item
            return group_layer(block_rows, lengths, bounds, weights)
        outputs, residual = lax.map(jax.checkpoint(one_group), (token_rows.reshape(groups, -1, D), seq_lengths.reshape(groups, SEQ_GRP), seg_bounds.reshape(groups, SEQ_GRP, LAND + 1)))
        return (outputs.reshape(token_rows.shape), residual.reshape(-1, HEADS))
    result, backward, residual = jax.vjp(forward, inputs, params, has_aux=True)
    grad_input, grads = backward(cotangent.astype(jnp.float32))
    return (result.astype(jnp.bfloat16), grad_input, grads[0], grads[1], grads[2], grads[3], grads[4], grads[5], grads[6], grads[7], grads[8], grads[9], grads[10], grads[11], grads[12], residual)
```

```python
import functools

import jax
import jax.numpy as jnp
from jax import lax
from jax.experimental import pallas as pl
from jax.experimental.pallas import tpu as pltpu
from jax.sharding import PartitionSpec as P

ITERS = 6
HALO = 16
PACK = 256
CHUNK = 256
CONV = 128
AXES = ("dp", "head")
F32 = jnp.float32
BF16 = jnp.bfloat16


def layer_norm(inputs, gains, offsets):
    centre = jnp.mean(inputs, axis=-1, keepdims=True)
    centred = inputs - centre
    spread = jnp.mean(centred * centred, axis=-1, keepdims=True)
    return centred * lax.rsqrt(spread + 1e-05) * gains + offsets


def gelu_exact(inputs):
    return 0.5 * inputs * (1.0 + jax.scipy.special.erf(inputs * 0.7071067811865476))


def pseudo_inverse(kernel):
    highest = lax.Precision.HIGHEST
    landmarks = kernel.shape[-1]
    identity = jnp.eye(landmarks, dtype=kernel.dtype)
    squares = jnp.sum(kernel * kernel, axis=(1, 2))
    inverse = jnp.swapaxes(kernel, 1, 2) / squares[:, None, None]
    for _ in range(ITERS):
        product = jnp.matmul(kernel, inverse, precision=highest)
        inner = 7.0 * identity - product
        inner = 15.0 * identity - jnp.matmul(product, inner, precision=highest)
        inner = 13.0 * identity - jnp.matmul(product, inner, precision=highest)
        inverse = 0.25 * jnp.matmul(inverse, inner, precision=highest)
    leftover = identity - jnp.matmul(kernel, inverse, precision=highest)
    residual = jnp.sqrt(jnp.sum(leftover * leftover, axis=(1, 2)) / landmarks)
    return (inverse, residual)


def landmark_inverse(q_land, k_land):
    scores = jnp.einsum("uhd,jhd->huj", q_land, k_land, precision=lax.Precision.HIGHEST)
    middle = jax.nn.softmax(scores * q_land.shape[-1] ** -0.5, axis=-1)
    return pseudo_inverse(middle)


def dot_nt(a, b):
    return lax.dot_general(a, b, (((1,), (1,)), ((), ())), preferred_element_type=F32)


def dot_tn(a, b):
    return lax.dot_general(a, b, (((0,), (0,)), ((), ())), preferred_element_type=F32)


def dot_nn(a, b):
    return lax.dot_general(a, b, (((1,), (0,)), ((), ())), preferred_element_type=F32)


def split(x):
    high = x.astype(BF16)
    return high, (x - high.astype(F32)).astype(BF16)


def same_head(dh):
    rows = lax.broadcasted_iota(jnp.int32, (PACK, PACK), 0) // dh
    cols = lax.broadcasted_iota(jnp.int32, (PACK, PACK), 1) // dh
    return rows == cols


def spread_heads(x, dh):
    tiled = jnp.concatenate([x] * (PACK // dh), axis=0)
    return jnp.where(same_head(dh), tiled, 0.0)


def gather_heads(full, dh):
    kept = jnp.where(same_head(dh), full, 0.0)
    total = kept[:dh]
    for part in range(1, PACK // dh):
        total = total + kept[part * dh : (part + 1) * dh]
    return total


def row_ids(start, rows, width):
    return start + lax.broadcasted_iota(jnp.int32, (rows, width), 0)


def group_max(x, dh):
    outs = []
    for t in range(x.shape[1] // 128):
        tile = x[:, t * 128 : (t + 1) * 128]
        left = lax.broadcasted_iota(jnp.int32, tile.shape, 1) < dh
        first = jnp.max(jnp.where(left, tile, -jnp.inf), axis=1, keepdims=True)
        second = jnp.max(jnp.where(left, -jnp.inf, tile), axis=1, keepdims=True)
        outs.append(jnp.where(left, first, second))
    return jnp.concatenate(outs, axis=1)


def scores_kernel(dh, count, q_ref, k_ref, v_ref, ql_ref, kl_ref, p1_ref, p3_ref, st_ref, s_ref):
    rows = q_ref.shape[0]
    steps = rows // CHUNK
    scale = dh**-0.5
    valid_rows = count[0]
    ql_high, ql_low = split(spread_heads(ql_ref[...] * scale, dh))
    kl_high, kl_low = split(spread_heads(kl_ref[...] * scale, dh))
    ones = jnp.where(same_head(dh), 1.0, 0.0).astype(BF16)

    def top(i, best):
        at = pl.ds(pl.multiple_of(i * CHUNK, CHUNK), CHUNK)
        k = k_ref[at, :]
        s = dot_nt(k, ql_high) + dot_nt(k, ql_low)
        s = jnp.where(row_ids(i * CHUNK, CHUNK, PACK) < valid_rows, s, -1e30)
        s_ref[at, :] = s
        return jnp.maximum(best, jnp.max(s, axis=0, keepdims=True))

    best = lax.fori_loop(0, steps, top, jnp.full((1, PACK), -1e30, F32))

    def weigh(i, carry):
        total, mixed = carry
        at = pl.ds(pl.multiple_of(i * CHUNK, CHUNK), CHUNK)
        e = jnp.exp(s_ref[at, :] - best)
        e = jnp.where(row_ids(i * CHUNK, CHUNK, PACK) < valid_rows, e, 0.0).astype(BF16)
        p3_ref[at, :] = e
        total = total + jnp.sum(e.astype(F32), axis=0, keepdims=True)
        return total, mixed + dot_tn(e, v_ref[at, :])

    total, mixed = lax.fori_loop(
        0, steps, weigh, (jnp.zeros((1, PACK), F32), jnp.zeros((PACK, PACK), F32))
    )
    st_ref[0:dh, :] = gather_heads(mixed, dh)
    eight = lax.broadcasted_iota(jnp.int32, (8, PACK), 0)
    st_ref[dh : dh + 8, :] = jnp.where(eight == 0, best, total)

    def first(i, carry):
        at = pl.ds(pl.multiple_of(i * CHUNK, CHUNK), CHUNK)
        q = q_ref[at, :]
        s = dot_nt(q, kl_high) + dot_nt(q, kl_low)
        e = jnp.exp(s - group_max(s, dh))
        norm = dot_nn(e.astype(BF16), ones)
        p1_ref[at, :] = (e / norm).astype(BF16)
        return carry

    lax.fori_loop(0, steps, first, 0)


def lanes_to_rows(row, dh):
    at = lax.broadcasted_iota(jnp.int32, (dh, PACK), 1) % dh
    diag = jnp.where(at == lax.broadcasted_iota(jnp.int32, (dh, PACK), 0), row, 0.0)
    ones = jnp.where(same_head(dh), 1.0, 0.0).astype(BF16)
    high = diag.astype(BF16)
    rest = diag - high.astype(F32)
    mid = rest.astype(BF16)
    low = (rest - mid.astype(F32)).astype(BF16)
    return dot_nn(high, ones) + dot_nn(mid, ones) + dot_nn(low, ones)


def join_stats(a, b, dh):
    top_a, top_b = a[dh : dh + 1], b[dh : dh + 1]
    top = jnp.maximum(top_a, top_b)
    wa, wb = jnp.exp(top_a - top), jnp.exp(top_b - top)
    total = a[dh + 1 : dh + 2] * wa + b[dh + 1 : dh + 2] * wb
    values = a[:dh] * lanes_to_rows(wa, dh) + b[:dh] * lanes_to_rows(wb, dh)
    return values, top, total


def join_kernel(dh, a_ref, b_ref, o_ref):
    for g in range(a_ref.shape[1] // PACK):
        at = slice(g * PACK, (g + 1) * PACK)
        values, top, total = join_stats(a_ref[:, at], b_ref[:, at], dh)
        o_ref[0:dh, at] = values
        eight = lax.broadcasted_iota(jnp.int32, (8, PACK), 0)
        o_ref[dh : dh + 8, at] = jnp.where(eight == 0, top, total)


def dot3(a, b, dot):
    ah, al = split(a)
    bh, bl = split(b)
    return dot(ah, bh) + dot(ah, bl) + dot(al, bh)


def mix_kernel(dh, a_ref, b_ref, mine_ref, z_ref, lv_ref, mixed_ref, scale_ref):
    for g in range(a_ref.shape[1] // PACK):
        at = slice(g * PACK, (g + 1) * PACK)
        values, top, total = join_stats(a_ref[:, at], b_ref[:, at], dh)
        inv = 1.0 / total
        lv = values * lanes_to_rows(inv, dh)
        lv_ref[:, at] = lv
        mixed_ref[:, at] = dot3(z_ref[:, at], spread_heads(lv, dh), dot_nn)
        scale = jnp.exp(mine_ref[dh : dh + 1, at] - top) * inv
        scale_ref[:, at] = jnp.broadcast_to(scale, (8, PACK))


def conv_block(t_ref, src_ref, block, dh):
    outs = []
    for pair in range(PACK // 128):
        lanes = slice(pair * 128, (pair + 1) * 128)
        rhs = src_ref[pl.ds(pl.multiple_of(block * CONV, CONV), CONV + 2 * HALO), lanes]
        lhs = t_ref[pair * 2 * CONV : (pair + 1) * 2 * CONV, :]
        both = dot_nn(lhs, rhs)
        left = lax.broadcasted_iota(jnp.int32, (CONV, 128), 1) < dh
        outs.append(jnp.where(left, both[:CONV], both[CONV:]))
    return jnp.concatenate(outs, axis=1)


def load_padded(pad_ref, before_ref, main_ref, after_ref):
    rows = main_ref.shape[0]
    pad_ref[0:HALO, :] = before_ref[...]
    pad_ref[HALO : HALO + rows, :] = main_ref[...]
    pad_ref[HALO + rows : HALO + rows + HALO, :] = after_ref[...]


def context_kernel(dh, count, p1_ref, v_ref, vb_ref, va_ref, mixed_ref, t_ref, o_ref, pad_ref):
    rows = p1_ref.shape[0]
    load_padded(pad_ref, vb_ref, v_ref, va_ref)
    mixed = spread_heads(mixed_ref[...], dh).astype(BF16)

    def step(i, carry):
        at = pl.ds(pl.multiple_of(i * CONV, CONV), CONV)
        total = dot_nn(p1_ref[at, :], mixed) + conv_block(t_ref, pad_ref, i, dh)
        total = jnp.where(row_ids(i * CONV, CONV, PACK) < count[0], total, 0.0)
        o_ref[at, :] = total.astype(BF16)
        return carry

    lax.fori_loop(0, rows // CONV, step, 0)


def mixed_grad_kernel(dh, p1_ref, d_ref, o_ref):
    steps = p1_ref.shape[0] // CHUNK

    def step(i, total):
        at = pl.ds(pl.multiple_of(i * CHUNK, CHUNK), CHUNK)
        return total + dot_tn(p1_ref[at, :], d_ref[at, :])

    o_ref[...] = gather_heads(lax.fori_loop(0, steps, step, jnp.zeros((PACK, PACK), F32)), dh)


def first_grad_kernel(
    dh, q_ref, d_ref, p1_ref, v_ref, vb_ref, va_ref, mixed_ref, kl_ref, dq_ref, dkl_ref, band_ref, pad_ref
):
    steps = p1_ref.shape[0] // CHUNK
    scale = dh**-0.5
    load_padded(pad_ref, vb_ref, v_ref, va_ref)
    mixed = spread_heads(mixed_ref[...], dh).astype(BF16)
    kl = spread_heads(kl_ref[...] * scale, dh).astype(BF16)
    ones = jnp.where(same_head(dh), 1.0, 0.0).astype(BF16)

    def step(i, total):
        at = pl.ds(pl.multiple_of(i * CHUNK, CHUNK), CHUNK)
        p1 = p1_ref[at, :].astype(F32)
        dp = dot_nt(d_ref[at, :], mixed)
        prod = p1 * dp
        high, low = split(prod)
        ds = (prod - p1 * (dot_nn(high, ones) + dot_nn(low, ones))).astype(BF16)
        dq_ref[at, :] = dot_nn(ds, kl)
        return total + dot_tn(ds, q_ref[at, :])

    total = lax.fori_loop(0, steps, step, jnp.zeros((PACK, PACK), F32))
    dkl_ref[...] = gather_heads(total, dh) * scale

    band_ref[...] = jnp.zeros_like(band_ref)

    def band(i, carry):
        at = pl.ds(pl.multiple_of(i * CONV, CONV), CONV)
        src = pl.ds(pl.multiple_of(i * CONV, CONV), CONV + 2 * HALO)
        for pair in range(PACK // 128):
            lanes = slice(pair * 128, (pair + 1) * 128)
            d = d_ref[at, lanes]
            left = lax.broadcasted_iota(jnp.int32, (CONV, 128), 1) < dh
            zero = jnp.zeros_like(d)
            both = jnp.concatenate([jnp.where(left, d, zero), jnp.where(left, zero, d)], axis=0)
            mine = slice(pair * 2 * CONV, (pair + 1) * 2 * CONV)
            band_ref[mine, :] += dot_nt(both, pad_ref[src, lanes])
        return carry

    lax.fori_loop(0, p1_ref.shape[0] // CONV, band, 0)


def last_grad_kernel(
    dh, count, k_ref, v_ref, p3_ref, d_ref, db_ref, da_ref, dlv_ref, lv_ref, scale_ref, ql_ref, t_ref,
    dk_ref, dv_ref, dql_ref, pad_ref
):
    rows = p3_ref.shape[0]
    scale = dh**-0.5
    load_padded(pad_ref, db_ref, d_ref, da_ref)
    row = scale_ref[0:1, :]
    dlv = (dlv_ref[...] * lanes_to_rows(row, dh)).astype(BF16)
    weight = spread_heads(dlv.astype(F32), dh).astype(BF16)
    prod = dlv.astype(F32) * lv_ref[...]
    high, low = split(spread_heads(prod, dh))
    ones = jnp.ones((8, PACK), BF16)
    offset = (dot_nt(ones, high) + dot_nt(ones, low))[0:1, :]
    ql = spread_heads(ql_ref[...] * scale, dh).astype(BF16)

    def step(i, total):
        at = pl.ds(pl.multiple_of(i * CONV, CONV), CONV)
        p3 = p3_ref[at, :]
        dp = dot_nt(v_ref[at, :], weight)
        ds = (p3.astype(F32) * (dp - offset)).astype(BF16)
        dk_ref[at, :] = dot_nn(ds, ql)
        dv = dot_nn(p3, weight) + conv_block(t_ref, pad_ref, i, dh)
        dv = jnp.where(row_ids(i * CONV, CONV, PACK) < count[0], dv, 0.0)
        dv_ref[at, :] = dv.astype(BF16)
        return total + dot_tn(ds, k_ref[at, :])

    total = lax.fori_loop(0, rows // CONV, step, jnp.zeros((PACK, PACK), F32))
    dql_ref[...] = gather_heads(total, dh) * scale


def call(kernel, name, grid, in_specs, out_specs, out_shape, scratch=(), flops=0, nbytes=0):
    return pl.pallas_call(
        kernel,
        name=name,
        grid_spec=pltpu.PrefetchScalarGridSpec(
            num_scalar_prefetch=1,
            grid=(grid,),
            in_specs=in_specs,
            out_specs=out_specs,
            scratch_shapes=list(scratch),
        ),
        out_shape=out_shape,
        cost_estimate=pl.CostEstimate(flops=flops, bytes_accessed=nbytes, transcendentals=0),
    )


def drop_count(kernel):
    def body(count, *refs):
        kernel(*refs)

    return body


def cols(rows, shift=0):
    return pl.BlockSpec((rows, PACK), lambda g, c: (0, g + shift))


def whole(shape):
    return pl.BlockSpec(shape, lambda g, c: (0,) * len(shape))


def struct(shape, dtype=F32):
    return jax.ShapeDtypeStruct(shape, dtype)


def swap(x, size, partner):
    return lax.ppermute(x, AXES, [(i, partner(i)) for i in range(size)])


def orders(size):
    bits = size.bit_length() - 1
    rest = list(range(1, bits))
    if len(rest) < 2:
        return [[0] + rest, [0] + rest]
    return [[0] + rest, [0, rest[1], rest[0]] + rest[2:]]


def my_bits(index, size):
    first, second = orders(size)
    odd = index & 1
    return [jnp.where(odd == 1, (index >> b) & 1, (index >> a) & 1) for a, b in zip(first, second)]


def partner_of(size, step):
    first, second = orders(size)
    return lambda i: i ^ (1 << (second[step] if i & 1 else first[step]))


def halves(x, bit):
    half = x.shape[0] // 2
    keep = lax.dynamic_slice_in_dim(x, bit * half, half, 0)
    send = lax.dynamic_slice_in_dim(x, (1 - bit) * half, half, 0)
    return keep, send


def reduce_scatter(keep, send, index, size):
    bits = my_bits(index, size)
    got = swap(send.astype(BF16), size, partner_of(size, 0))
    total = keep.astype(F32) + got.astype(F32)
    for step in range(1, len(bits)):
        keep, send = halves(total, bits[step])
        got = swap(send.astype(BF16), size, partner_of(size, step))
        total = keep + got.astype(F32)
    return total


def gather_back(part, index, size):
    bits = my_bits(index, size)
    part = part.astype(BF16)
    for step in reversed(range(len(bits))):
        got = swap(part, size, partner_of(size, step))
        low = jnp.where(bits[step] == 0, part, got)
        high = jnp.where(bits[step] == 0, got, part)
        part = jnp.concatenate([low, high], axis=0)
    return part


def sum_all(x, size):
    for bit in range(size.bit_length() - 1):
        x = x + swap(x, size, lambda i: i ^ (1 << bit))
    return x


def body(
    tokens,
    seq_lengths,
    seg_bounds,
    w_qkv,
    b_qv,
    conv_w,
    w_out,
    b_out,
    ln1_gain,
    ln1_bias,
    w_up,
    b_up,
    w_down,
    b_down,
    ln2_gain,
    ln2_bias,
    cotangent,
):
    rows, width = tokens.shape
    group = lax.axis_size("head")
    size = lax.axis_size("dp") * group
    head_index = lax.axis_index("head")
    index = lax.axis_index(AXES)
    hidden_width = w_up.shape[1]
    heads_local = conv_w.shape[0]
    heads = heads_local * group
    taps = conv_w.shape[1]
    dh = width // heads
    lands = seg_bounds.shape[1] - 1
    packs = width // PACK
    assert seq_lengths.shape[0] == 1 and lands == dh == 64 and taps == 2 * HALO + 1

    def group_step(x, bit):
        return swap(x, size, lambda i: i ^ bit)

    length = seq_lengths[0]
    bounds = seg_bounds[0]
    start = head_index * rows
    count = jnp.clip(length - start, 0, rows).reshape(1).astype(jnp.int32)
    position = start + jnp.arange(rows, dtype=jnp.int32)
    valid = (position < length).astype(F32)
    member = (position[None, :] >= bounds[:-1, None]) & (position[None, :] < bounds[1:, None])
    member_low = member.astype(BF16)
    widths = (bounds[1:] - bounds[:-1]).astype(F32)

    all_taps = lax.dynamic_update_slice(
        jnp.zeros((heads, taps), F32), conv_w, (head_index * heads_local, 0)
    )
    all_taps = all_taps + group_step(all_taps, 2)
    all_taps = all_taps + group_step(all_taps, 1)

    def banded(w):
        span = CONV + 2 * HALO
        padded = jnp.pad(w, ((0, 0), (0, span + 1 - taps)))
        tiled = jnp.tile(padded, (1, CONV))[:, : CONV * span]
        return tiled.reshape(heads * CONV, span).astype(BF16)

    band_fwd = banded(all_taps)
    band_bwd = banded(all_taps[:, ::-1])

    qkv_bias = jnp.concatenate([b_qv[:width], jnp.zeros((width,), F32), b_qv[width:]])
    projected = jnp.dot(tokens, w_qkv, preferred_element_type=F32) + qkv_bias
    keep = (jnp.arange(3 * width) < 2 * width)[None, :] | (valid[:, None] > 0.0)
    projected = jnp.where(keep, projected, 0.0).astype(BF16)

    land = jnp.dot(member_low, projected[:, : 2 * width], preferred_element_type=F32)
    land = land + group_step(land, 2)
    land = land + group_step(land, 1)
    land = land / widths[:, None]
    q_land, k_land = land[:, :width], land[:, width:]

    v_edge_low = projected[:HALO, 2 * width :]
    v_edge_high = projected[rows - HALO :, 2 * width :]
    forth = [(d * group + i, d * group + i + 1) for d in range(size // group) for i in range(group - 1)]
    back = [(b, a) for a, b in forth]
    v_before = lax.ppermute(v_edge_high, AXES, forth)
    v_after = lax.ppermute(v_edge_low, AXES, back)

    flop = 2 * rows * width * PACK
    p_first, p_last, stats = call(
        lambda c, *refs: scores_kernel(dh, c, *refs),
        "scores",
        packs,
        [cols(rows), cols(rows, packs), cols(rows, 2 * packs), cols(dh), cols(dh)],
        [cols(rows), cols(rows), cols(dh + 8)],
        [struct((rows, width), BF16), struct((rows, width), BF16), struct((dh + 8, width))],
        [pltpu.VMEM((rows, PACK), F32)],
        6 * flop,
        rows * width * 10,
    )(count, projected, projected, projected, q_land, k_land)

    def own_heads(x):
        mine = lax.dynamic_slice_in_dim(x, head_index * heads_local * dh, heads_local * dh, 1)
        return mine.reshape(lands, heads_local, dh)

    inverse, inverse_back, residual = jax.vjp(
        landmark_inverse, own_heads(q_land), own_heads(k_land), has_aux=True
    )

    def place_own(x, total):
        flat = x.reshape(lands, heads_local * dh)
        return lax.dynamic_update_slice_in_dim(total, flat, head_index * heads_local * dh, 1)

    z_all = place_own(jnp.swapaxes(inverse, 0, 1), jnp.zeros((lands, width), F32))
    z_all = z_all + group_step(z_all, 2)
    z_all = z_all + group_step(z_all, 1)

    other = group_step(stats, 2)
    joined = call(
        drop_count(functools.partial(join_kernel, dh)),
        "join",
        1,
        [whole(stats.shape)] * 2,
        whole(stats.shape),
        struct(stats.shape),
        flops=1000,
        nbytes=6 * stats.size,
    )(count, stats, other)
    other = group_step(joined, 1)
    lv, mixed, last_scale = call(
        drop_count(functools.partial(mix_kernel, dh)),
        "mix",
        1,
        [whole(stats.shape)] * 3 + [whole((lands, width))],
        [whole((lands, width)), whole((lands, width)), whole((8, width))],
        [struct((lands, width)), struct((lands, width)), struct((8, width))],
        flops=1000,
        nbytes=6 * stats.size,
    )(count, joined, other, stats, z_all)

    halo = pl.BlockSpec((HALO, PACK), lambda g, c: (0, g))
    span = CONV + 2 * HALO
    band_spec = pl.BlockSpec((PACK // dh * CONV, span), lambda g, c: (g, 0))
    padded = pltpu.VMEM((rows + 2 * HALO, PACK), BF16)
    context = call(
        lambda c, *refs: context_kernel(dh, c, *refs),
        "context",
        packs,
        [cols(rows), cols(rows, 2 * packs), halo, halo, cols(dh), band_spec],
        cols(rows),
        struct((rows, width), BF16),
        [padded],
        3 * flop,
        rows * width * 6,
    )(count, p_first, projected, v_before, v_after, mixed, band_fwd)

    attn_out = jnp.dot(context, w_out, preferred_element_type=F32) + b_out
    normed, norm1_back = jax.vjp(layer_norm, tokens.astype(F32) + attn_out, ln1_gain, ln1_bias)
    normed_low = normed.astype(BF16)
    upper = jnp.dot(normed_low, w_up, preferred_element_type=F32) + b_up
    activated, gelu_back = jax.vjp(gelu_exact, upper)
    act_low = activated.astype(BF16)
    ffn_out = jnp.dot(act_low, w_down, preferred_element_type=F32) + b_down
    final, norm2_back = jax.vjp(layer_norm, normed + ffn_out, ln2_gain, ln2_bias)
    result = (final * valid[:, None]).astype(BF16)
    d_final = cotangent.astype(F32) * valid[:, None]
    d_sum, d_gain_two, d_bias_two = norm2_back(d_final)
    d_ffn = d_sum.astype(BF16)

    first_bit = my_bits(index, size)[0]

    def weight_grad(left, right):
        keep, send = halves(left.T, first_bit)
        send = jnp.dot(send, right, preferred_element_type=F32).astype(BF16)
        return jnp.dot(keep, right, preferred_element_type=F32).astype(BF16), send

    def reduced(left, right):
        keep, send = weight_grad(left, right)
        return gather_back(reduce_scatter(keep, send, index, size), index, size)

    full_down = reduced(act_low, d_ffn).astype(F32)
    gb_down = jnp.sum(d_ffn.astype(F32), axis=0)
    d_act = jnp.einsum("td,kd->tk", d_ffn, w_down, preferred_element_type=F32)
    (d_upper,) = gelu_back(d_act)
    d_upper_low = d_upper.astype(BF16)
    gb_up = jnp.sum(d_upper_low.astype(F32), axis=0)
    d_normed = d_sum + jnp.einsum("tk,dk->td", d_upper_low, w_up, preferred_element_type=F32)
    d_resid, d_gain_one, d_bias_one = norm1_back(d_normed)
    d_attn = d_resid.astype(BF16)
    full_up = reduced(normed_low, d_upper_low).astype(F32)
    full_out = reduced(context, d_attn).astype(F32)
    gb_out = jnp.sum(d_attn.astype(F32), axis=0)
    d_context = jnp.einsum("te,de->td", d_attn, w_out, preferred_element_type=F32)
    d_context = (d_context * valid[:, None]).astype(BF16)

    d_before = lax.ppermute(d_context[rows - HALO :], AXES, forth)
    d_after = lax.ppermute(d_context[:HALO], AXES, back)
    d_mixed = call(
        drop_count(functools.partial(mixed_grad_kernel, dh)),
        "mixed_grad",
        packs,
        [cols(rows), cols(rows)],
        cols(dh),
        struct((lands, width)),
        flops=flop,
        nbytes=rows * width * 4,
    )(count, p_first, d_context)
    d_mixed = d_mixed + group_step(d_mixed, 2)
    d_mixed = d_mixed + group_step(d_mixed, 1)

    dq_own, dkl_part, band = call(
        drop_count(functools.partial(first_grad_kernel, dh)),
        "first_grad",
        packs,
        [cols(rows), cols(rows), cols(rows), cols(rows, 2 * packs), halo, halo, cols(dh), cols(dh)],
        [cols(rows), cols(dh), band_spec],
        [struct((rows, width)), struct((lands, width)), struct((heads * CONV, span))],
        [padded],
        6 * flop,
        rows * width * 12,
    )(count, projected, d_context, p_first, projected, v_before, v_after, mixed, k_land)

    by_head = lambda x: x.reshape(lands, heads, dh)
    highest = lax.Precision.HIGHEST
    d_lv = jnp.einsum("uhj,uhd->jhd", by_head(z_all), by_head(d_mixed), precision=highest)
    d_lv = d_lv.reshape(lands, width)
    d_inverse = jnp.einsum("uhd,jhd->huj", own_heads(d_mixed), own_heads(lv), precision=highest)
    dql_mid, dkl_mid = inverse_back(d_inverse)

    dk_own, dv, dql_part = call(
        lambda c, *refs: last_grad_kernel(dh, c, *refs),
        "last_grad",
        packs,
        [
            cols(rows, packs), cols(rows, 2 * packs), cols(rows), cols(rows), halo, halo,
            cols(dh), cols(dh), cols(8), cols(dh), band_spec,
        ],
        [cols(rows), cols(rows), cols(dh)],
        [struct((rows, width)), struct((rows, width), BF16), struct((lands, width))],
        [padded],
        6 * flop,
        rows * width * 14,
    )(count, projected, projected, p_last, d_context, d_before, d_after, d_lv, lv, last_scale, q_land, band_bwd)

    zeros = jnp.zeros((lands, width), F32)
    d_land = jnp.concatenate(
        [dql_part + place_own(dql_mid, zeros), dkl_part + place_own(dkl_mid, zeros)], axis=1
    )
    d_land = d_land / widths[:, None]
    d_land = d_land + group_step(d_land, 2)
    d_land = d_land + group_step(d_land, 1)
    d_qk = jnp.dot(member_low.T, d_land.astype(BF16), preferred_element_type=F32)
    d_q = (dq_own + d_qk[:, :width]).astype(BF16)
    d_k = (dk_own + d_qk[:, width:]).astype(BF16)
    d_proj = jnp.concatenate([d_q, d_k, dv], axis=1)

    full_qkv = reduced(tokens, d_proj).astype(F32)
    proj_sums = jnp.sum(d_proj.astype(F32), axis=0)
    gb_qv = jnp.concatenate([proj_sums[:width], proj_sums[2 * width :]])
    d_tokens = d_resid + jnp.einsum("tk,dk->td", d_proj, w_qkv, preferred_element_type=F32)

    flat = jnp.pad(band.reshape(heads, CONV * span), ((0, 0), (0, CONV)))
    d_taps = jnp.sum(flat.reshape(heads, CONV, span + 1), axis=1)[:, :taps]
    small = jnp.concatenate(
        [gb_qv, gb_out, d_gain_one, d_bias_one, gb_up, gb_down, d_gain_two, d_bias_two, d_taps.reshape(-1)]
    )
    pad = -small.shape[0] % 1024
    small = sum_all(jnp.pad(small, (0, pad)).reshape(-1, 128), size).reshape(-1)
    ends = [0]
    for n in (2 * width, width, width, width, hidden_width, width, width, width, heads * taps):
        ends.append(ends[-1] + n)
    pieces = [small[a:b] for a, b in zip(ends, ends[1:])]
    g_taps = lax.dynamic_slice_in_dim(
        pieces[8].reshape(heads, taps), head_index * heads_local, heads_local, 0
    )
    return (
        result,
        d_tokens,
        full_qkv,
        pieces[0],
        g_taps,
        full_out,
        pieces[1],
        pieces[2],
        pieces[3],
        full_up,
        pieces[4],
        full_down,
        pieces[5],
        pieces[6],
        pieces[7],
        residual.reshape(1, heads_local),
    )


def solution(mesh):
    tokens = P(AXES, None)
    copied = [P()] * 10
    return jax.shard_map(
        body,
        mesh=mesh,
        in_specs=(tokens, P("dp"), P("dp", None), P(), P(), P("head", None), *copied, tokens),
        out_specs=(tokens, tokens, P(), P(), P("head", None), *copied, P("dp", "head")),
        check_vma=False,
    )
```
